32 devices in a mesh: ctx: 4 (over y, core), shard: 8 (over z, x).
Axes of the slice: x: 2, y: 2, z: 4, core: 2. Of those that a mesh axis runs over, the one named last changes fastest.
Arguments:
- block_input: bfloat16 [8, 1024, 1024], P('shard', 'ctx'), may hold values from -6 to 6
- lengths: int32 [8], P('shard'), may hold values from 256 to 1024, as said below
- mem_keep: float32 [8, 8], P('shard', 'ctx'), may hold values from 0.9 to 0.999
- mem_momentum: float32 [8, 8], P('shard', 'ctx'), may hold values from 0.5 to 0.8
- mem_rate: float32 [8, 8], P('shard', 'ctx'), may hold values from 0.002 to 0.01
- norm_gain: bfloat16 [1024], P('shard'), may hold values from 0.5 to 1.5
- w_query: bfloat16 [1024, 1024], P('shard'), may hold values from -0.1875 to 0.1875
- w_key: bfloat16 [1024, 1024], P('shard'), may hold values from -0.1875 to 0.1875
- w_value: bfloat16 [1024, 1024], P('shard'), may hold values from -0.1875 to 0.1875
- persist_keys: bfloat16 [16, 1024], P(None, 'shard'), may hold values from -6 to 6
- persist_values: bfloat16 [16, 1024], P(None, 'shard'), may hold values from -6 to 6
- w_out: bfloat16 [1024, 1024], P('shard'), may hold values from -6 to 6
- mem_query: bfloat16 [1024, 1024], P('shard'), may hold values from -0.1875 to 0.1875
- mem_key: bfloat16 [1024, 1024], P('shard'), may hold values from -0.1875 to 0.1875
- mem_value: bfloat16 [1024, 1024], P('shard'), may hold values from -0.1875 to 0.1875
- mem_first: bfloat16 [1024, 1024], P('shard'), may hold values from -0.1875 to 0.1875
- mem_second: bfloat16 [1024, 1024], P('shard'), may hold values from -0.1875 to 0.1875
- ffn_gain: bfloat16 [1024], P('shard'), may hold values from 0.5 to 1.5
- w_gate: bfloat16 [1024, 2816], P('shard'), may hold values from -0.1875 to 0.1875
- w_up: bfloat16 [1024, 2816], P('shard'), may hold values from -0.1875 to 0.1875
- w_down: bfloat16 [2816, 1024], P('shard'), may hold values from -0.109375 to 0.109375
- cotangent: bfloat16 [8, 1024, 1024], P('shard', 'ctx'), may hold values from -6 to 6
Outputs:
- output: bfloat16 [8, 1024, 1024], P('shard', 'ctx')
- input_grad: bfloat16 [8, 1024, 1024], P('shard', 'ctx')
- grad_norm_gain: float32 [1024], P(('ctx', 'shard'))
- grad_w_query: float32 [1024, 1024], P(('ctx', 'shard'))
- grad_w_key: float32 [1024, 1024], P(('ctx', 'shard'))
- grad_w_value: float32 [1024, 1024], P(('ctx', 'shard'))
- grad_persist_keys: float32 [16, 1024], P(None, ('ctx', 'shard'))
- grad_persist_values: float32 [16, 1024], P(None, ('ctx', 'shard'))
- grad_w_out: float32 [1024, 1024], P(('ctx', 'shard'))
- grad_mem_query: float32 [1024, 1024], P(('ctx', 'shard'))
- grad_mem_key: float32 [1024, 1024], P(('ctx', 'shard'))
- grad_mem_value: float32 [1024, 1024], P(('ctx', 'shard'))
- grad_mem_first: float32 [1024, 1024], P(('ctx', 'shard'))
- grad_mem_second: float32 [1024, 1024], P(('ctx', 'shard'))
- grad_ffn_gain: float32 [1024], P(('ctx', 'shard'))
- grad_w_gate: float32 [1024, 2816], P(('ctx', 'shard'))
- grad_w_up: float32 [1024, 2816], P(('ctx', 'shard'))
- grad_w_down: float32 [2816, 1024], P(('ctx', 'shard'))
The draws below stay inside these ranges and needn't reach their ends.
Inputs may be any that keep to these rules, and one draw needn't show every extreme that they name: `lengths`: each length is a multiple of 128; in every draw some sequence has length 1024.
All inputs are finite; a program needn't handle non-finite values.
Results may differ from the reference program's by a relative error of at most 0.02.
Values may be sent and summed in bfloat16 or wider, within the bound.
No kernel may reach another device: no remote copies, remote signals or barrier semaphores. Data moves between devices by JAX's collectives and lax.ppermute only.
A program may use at most 512 MiB of HBM per device.

```python
import math
import jax
import jax.numpy as jnp
from jax import lax

D = 1024
HEADS = 8
HEAD_DIM = 128
FF = 2816
MH = 1024
NP = 16
WINDOW = 1024
SPAN = 128
LEN = 1024
SEQS = 8
NCH = 8


def draw_lengths(key, part):
    first_key, second_key = jax.random.split(key)
    blocks = jax.random.randint(first_key, (SEQS,), LEN // (4 * SPAN), LEN // SPAN + 1)
    longest = jax.random.randint(second_key, (), 0, SEQS)
    blocks = jnp.where(jnp.arange(SEQS) == longest, LEN // SPAN, blocks)
    return (blocks * SPAN).astype(jnp.int32)


def block_levels(own_key, extent, cuts, smallest, largest):
    level, own = 1.0, jax.random.fold_in(own_key, 6)
    for dim, blocks in cuts:
        draws = jnp.exp(jax.random.uniform(jax.random.fold_in(own, dim), (blocks,), jnp.float32, smallest / len(cuts), largest / len(cuts)))
        level = level * jnp.repeat(draws, extent[dim] // blocks).reshape([-1 if axis == dim else 1 for axis in range(len(extent))])
    return level


def centred(key, extent, spread, reach, cuts=(), held_as=jnp.bfloat16):
    drawn = jax.random.normal(key, extent, jnp.float32) * spread
    if len(cuts) > 0:
        drawn = block_levels(key, extent, cuts, -0.22, 0.18) * drawn
    return jnp.clip(drawn, min=-reach, max=reach).astype(held_as)


def setup_inputs(seed: int = 0) -> dict:
    key_of = jax.random.split(jax.random.key(seed), 23)
    block_input = centred(key_of[0], (SEQS, LEN, D), 1.0, 6.0, ((0, 8), (1, 4)))
    lengths = draw_lengths(jax.random.fold_in(key_of[22], 71), 0)
    mem_keep = jnp.clip(0.9 + 0.09900004 * jax.random.uniform(key_of[2], (SEQS, NCH), jnp.float32) ** block_levels(key_of[2], (SEQS, NCH), ((0, 8), (1, 4)), -0.2, 0.2), 0.9, 0.999)
    mem_momentum = jnp.clip(0.5 + 0.3 * jax.random.uniform(key_of[3], (SEQS, NCH), jnp.float32) ** block_levels(key_of[3], (SEQS, NCH), ((0, 8), (1, 4)), -0.2, 0.2), 0.5, 0.8)
    mem_rate = jnp.clip(jnp.exp(math.log(0.01) - 1.6094378 * jax.random.uniform(key_of[4], (SEQS, NCH), jnp.float32) ** block_levels(key_of[4], (SEQS, NCH), ((0, 8), (1, 4)), -0.2, 0.2)), 0.002, 0.01)
    norm_gain = jnp.clip(1.0 + 0.1 * jax.random.normal(key_of[5], (D,), jnp.float32), 0.5, 1.5).astype(jnp.bfloat16)
    w_query = centred(key_of[6], (D, D), D ** -0.5, 0.1875, ((0, 8),))
    w_key = centred(key_of[7], (D, D), D ** -0.5, 0.1875, ((0, 8),))
    w_value = centred(key_of[8], (D, D), D ** -0.5, 0.1875, ((0, 8),))
    persist_keys = centred(key_of[9], (NP, D), 1.0, 6.0, ((1, 8),))
    persist_values = centred(key_of[10], (NP, D), 1.0, 6.0, ((1, 8),))
    w_out = centred(key_of[11], (D, D), 1 ** -0.5, 6.0, ((0, 8),))
    mem_query = centred(key_of[12], (D, D), D ** -0.5, 0.1875, ((0, 8),))
    mem_key = centred(key_of[13], (D, D), D ** -0.5, 0.1875, ((0, 8),))
    mem_value = centred(key_of[14], (D, D), D ** -0.5, 0.1875, ((0, 8),))
    mem_first = centred(key_of[15], (D, MH), D ** -0.5, 0.1875, ((0, 8),))
    mem_second = centred(key_of[16], (MH, D), MH ** -0.5, 0.1875, ((0, 8),))
    ffn_gain = jnp.clip(1.0 + 0.1 * jax.random.normal(key_of[17], (D,), jnp.float32), 0.5, 1.5).astype(jnp.bfloat16)
    w_gate = centred(key_of[18], (D, FF), D ** -0.5, 0.1875, ((0, 8),))
    w_up = centred(key_of[19], (D, FF), D ** -0.5, 0.1875, ((0, 8),))
    w_down = centred(key_of[20], (FF, D), FF ** -0.5, 0.109375, ((0, 8),))
    cotangent = centred(key_of[21], (SEQS, LEN, D), 1.0, 6.0, ((0, 8), (1, 4)))
    return dict(block_input=block_input, lengths=lengths, mem_keep=mem_keep, mem_momentum=mem_momentum, mem_rate=mem_rate, norm_gain=norm_gain, w_query=w_query, w_key=w_key, w_value=w_value, persist_keys=persist_keys, persist_values=persist_values, w_out=w_out, mem_query=mem_query, mem_key=mem_key, mem_value=mem_value, mem_first=mem_first, mem_second=mem_second, ffn_gain=ffn_gain, w_gate=w_gate, w_up=w_up, w_down=w_down, cotangent=cotangent)


@jax.custom_vjp
def low(v):
    return lax.optimization_barrier(v.astype(jnp.bfloat16)).astype(jnp.float32)

@jax.custom_vjp
def low_back(v):
    return v

def low_keep(v):
    return (low(v), None)

def low_pass(kept, grad):
    return (grad,)

def back_keep(v):
    return (v, None)

def back_low(kept, grad):
    return (low(grad),)
low.defvjp(low_keep, low_pass)
low_back.defvjp(back_keep, back_low)
highest = lax.Precision.HIGHEST

def matmul(left, right):
    return jnp.dot(left, right, precision=highest)

def rms_norm(values, gain):
    return values * lax.rsqrt(lax.optimization_barrier(jnp.mean(values * values, axis=-1, keepdims=True)) + 1e-05) * gain

def silu_slope(inputs):
    sigma = jax.nn.sigmoid(inputs)
    return sigma * (1.0 + inputs * (1.0 - sigma))

def memory_span(state, inputs):
    first, second, speed_first, speed_second = state
    query_rows, key_rows, value_rows, alive, keep, momentum, rate = inputs
    recalled = matmul(jax.nn.silu(matmul(query_rows, first)), second)
    hidden_pre = matmul(key_rows, first)
    hidden_act = jax.nn.silu(hidden_pre)
    error = (matmul(hidden_act, second) - value_rows) * alive[:, None] / SPAN
    grad_second = matmul(hidden_act.T, error)
    grad_first = matmul(key_rows.T, matmul(error, second.T) * silu_slope(hidden_pre))
    speed_first = momentum * speed_first - rate * grad_first
    speed_second = momentum * speed_second - rate * grad_second
    first = keep * first + speed_first
    second = keep * second + speed_second
    return ((first, second, speed_first, speed_second), recalled)

def memory_segment(state, query_rows, key_rows, value_rows, alive, keep, momentum, rate):
    count = alive.shape[0] // SPAN
    shaped = (query_rows.reshape(count, SPAN, -1), key_rows.reshape(count, SPAN, -1), value_rows.reshape(count, SPAN, -1), alive.reshape(count, SPAN), keep, momentum, rate)
    state, recalled = lax.scan(jax.checkpoint(memory_span), state, shaped)
    return (state, recalled.reshape(alive.shape[0], -1))

def attention(queries, keys, values, pkeys, pvalues, alive):
    slots = jnp.arange(LEN)
    query_heads = queries.reshape(LEN, HEADS, HEAD_DIM)
    key_heads = jnp.concatenate([pkeys, keys], 0).reshape(NP + LEN, HEADS, HEAD_DIM)
    value_heads = jnp.concatenate([pvalues, values], 0).reshape(NP + LEN, HEADS, HEAD_DIM)
    scores = jnp.einsum('thd,shd->hts', query_heads, key_heads, precision=highest) * HEAD_DIM ** (-0.5)
    scores = low_back(scores)
    window_ok = (slots[None, :] <= slots[:, None]) & (slots[:, None] - slots[None, :] < WINDOW) & (alive[None, :] > 0.5)
    allowed = jnp.concatenate([jnp.ones((LEN, NP), dtype=bool), window_ok], 1)
    scores = jnp.where(allowed[None], scores, -1e+30)
    probs = low(jax.nn.softmax(scores, axis=-1))
    mixed = jnp.einsum('hts,shd->thd', probs, value_heads, precision=highest)
    return low_back(mixed.reshape(LEN, D))

def layer(tokens, params, alive, keep, momentum, rate):
    norm_gain, w_query, w_key, w_value, persist_keys, persist_values, w_out, mem_query, mem_key, mem_value, mem_first, mem_second, ffn_gain, w_gate, w_up, w_down = params
    normed = low(rms_norm(tokens, norm_gain))
    queries = low_back(low(matmul(normed, w_query)))
    keys = low_back(low(matmul(normed, w_key)))
    values = low_back(low(matmul(normed, w_value)))
    attended = attention(queries, keys, values, low(persist_keys), low(persist_values), alive)
    mquery = low_back(low(matmul(normed, mem_query)))
    mkey = low_back(low(matmul(normed, mem_key)))
    mvalue = low_back(low(matmul(normed, mem_value)))
    start = (mem_first, mem_second, jnp.zeros_like(mem_first), jnp.zeros_like(mem_second))
    _, recalled = memory_segment(start, mquery, mkey, mvalue, alive, keep, momentum, rate)
    combined = low(attended * recalled)
    middle = tokens + low_back(matmul(combined, w_out))
    normed_two = low(rms_norm(middle, ffn_gain))
    gate = low_back(matmul(normed_two, w_gate))
    upper = low_back(matmul(normed_two, w_up))
    activated = low(jax.nn.silu(gate) * upper)
    ffn_out = low_back(matmul(activated, w_down))
    return alive[:, None] * (middle + ffn_out)

def reference(block_input, lengths, mem_keep, mem_momentum, mem_rate, norm_gain, w_query, w_key, w_value, persist_keys, persist_values, w_out, mem_query, mem_key, mem_value, mem_first, mem_second, ffn_gain, w_gate, w_up, w_down, cotangent):
    params = tuple((p.astype(jnp.float32) for p in (norm_gain, w_query, w_key, w_value, persist_keys, persist_values, w_out, mem_query, mem_key, mem_value, mem_first, mem_second, ffn_gain, w_gate, w_up, w_down)))

    def one_sequence(totals, sequence_inputs):
        tokens, length, keep, momentum, rate, cot = sequence_inputs
        alive = (jnp.arange(LEN) < length).astype(jnp.float32)
        result, pull = jax.vjp(lambda tok_in, par_in: layer(tok_in, par_in, alive, keep, momentum, rate), tokens.astype(jnp.float32), params)
        d_tokens, d_params = pull(cot.astype(jnp.float32))
        totals = jax.tree.map(jnp.add, totals, d_params)
        return (totals, (result.astype(jnp.bfloat16), d_tokens.astype(jnp.bfloat16)))
    start = tuple((jnp.zeros_like(p) for p in params))
    totals, (outputs, grads_in) = lax.scan(one_sequence, start, (block_input, lengths, mem_keep, mem_momentum, mem_rate, cotangent))
    return (outputs, grads_in, totals[0], totals[1], totals[2], totals[3], totals[4], totals[5], totals[6], totals[7], totals[8], totals[9], totals[10], totals[11], totals[12], totals[13], totals[14], totals[15])
```

```python
import jax
import jax.numpy as jnp
from jax import lax
from jax.sharding import PartitionSpec as P

HEADS = 8
HEAD_DIM = 128
WINDOW = 1024
SPAN = 128
EPS = 1e-05
bf16 = jnp.bfloat16
f32 = jnp.float32


def split_axis(size, inner):
    return size // inner, inner


def shard_inner(size):
    inner = 1
    while inner * inner * 4 <= size:
        inner *= 2
    return inner


def dot(left, right):
    return jnp.dot(left, right, preferred_element_type=f32)


def dot_t(left, right):
    return lax.dot_general(left, right, (((1,), (1,)), ((), ())), preferred_element_type=f32)


def t_dot(left, right):
    return lax.dot_general(left, right, (((0,), (0,)), ((), ())), preferred_element_type=f32)


def line_place(axis, stride, count):
    return (lax.axis_index(axis) // stride) % count


def shift(value, axis, stride, count, step):
    size = lax.axis_size(axis)
    pairs = [
        (i, i + step * stride) for i in range(size) if 0 <= (i // stride) % count + step < count
    ]
    return lax.ppermute(value, axis, pairs)


def swap(value, axis, stride):
    size = lax.axis_size(axis)
    return lax.ppermute(value, axis, [(i, i ^ stride) for i in range(size)])


def line_gather(value, axis, stride, count):
    if count == 1:
        return value[None]
    place = line_place(axis, stride, count)
    if count == 2:
        other = swap(value, axis, stride)
        return jnp.stack([jnp.where(place == 0, value, other), jnp.where(place == 0, other, value)])
    below, above = [], []
    low = high = value
    for _ in range(count - 1):
        low = shift(low, axis, stride, count, 1)
        high = shift(high, axis, stride, count, -1)
        below.append(low)
        above.append(high)
    every = jnp.stack(below[::-1] + [value] + above)
    return lax.dynamic_slice_in_dim(every, count - 1 - place, count, 0)


def line_reduce(blocks, axis, stride, count):
    if count == 1:
        return blocks[0]
    place = line_place(axis, stride, count)

    def own(index):
        return lax.dynamic_index_in_dim(blocks, index, 0, keepdims=False)

    if count == 2:
        return own(place) + swap(own(1 - place).astype(bf16), axis, stride).astype(f32)
    right = left = None
    for step in range(1, count):
        send_right = own(jnp.clip(place + count - step, 0, count - 1))
        send_left = own(jnp.clip(place - count + step, 0, count - 1))
        if right is not None:
            send_right = send_right + right.astype(f32)
            send_left = send_left + left.astype(f32)
        right = shift(send_right.astype(bf16), axis, stride, count, 1)
        left = shift(send_left.astype(bf16), axis, stride, count, -1)
    return own(place) + right.astype(f32) + left.astype(f32)


def gather_ctx(value):
    size = lax.axis_size("ctx")
    outer, inner = split_axis(size, 2 if size % 2 == 0 else 1)
    columns = line_gather(value, "ctx", inner, outer)
    both = line_gather(columns, "ctx", 1, inner)
    both = jnp.swapaxes(both, 0, 1)
    return both.reshape((size * value.shape[0],) + value.shape[1:])


def reduce_ctx(value):
    size = lax.axis_size("ctx")
    outer, inner = split_axis(size, 2 if size % 2 == 0 else 1)
    blocks = value.reshape((outer, inner, value.shape[0] // size) + value.shape[1:])
    kept = line_reduce(jnp.swapaxes(blocks, 0, 1), "ctx", 1, inner)
    return line_reduce(kept, "ctx", inner, outer)


def gather_shard(value):
    size = lax.axis_size("shard")
    outer, inner = split_axis(size, shard_inner(size))
    columns = line_gather(value, "shard", inner, outer)
    both = line_gather(columns, "shard", 1, inner)
    both = jnp.swapaxes(both, 0, 1)
    return both.reshape((size,) + value.shape)


def reduce_shard(value):
    size = lax.axis_size("shard")
    outer, inner = split_axis(size, shard_inner(size))
    blocks = value.reshape((outer, inner) + value.shape[1:])
    kept = line_reduce(jnp.swapaxes(blocks, 0, 1), "shard", 1, inner)
    return line_reduce(kept, "shard", inner, outer)


def rms_rows(values):
    return lax.rsqrt(jnp.mean(values * values, axis=-1, keepdims=True) + EPS)


def rms_back(values, root, gain, grad):
    scaled = grad * gain
    mean = jnp.mean(values * scaled, axis=-1, keepdims=True)
    return root * scaled - values * (root * root * root * mean), jnp.sum(grad * values * root, axis=0)


def silu_parts(z):
    s = jax.nn.sigmoid(z)
    slope = s * (1.0 + z * (1.0 - s))
    bend = s * (1.0 - s) * (2.0 + z * (1.0 - 2.0 * s))
    return z * s, slope, bend


def tables(keep, momentum, rate):
    count = keep.shape[0]
    a = jnp.ones((), f32)
    b = jnp.zeros((count,), f32)
    m = jnp.zeros((count,), f32)
    spot = jnp.arange(count)
    all_a, all_b = [], []
    for c in range(count):
        all_a.append(a)
        all_b.append(b)
        m = momentum[c] * m + jnp.where(spot == c, rate[c], 0.0)
        b = keep[c] * b + m
        a = keep[c] * a
    return jnp.stack(all_a), jnp.stack(all_b)


def on_device(
    block_input, lengths, mem_keep, mem_momentum, mem_rate, norm_gain, w_query, w_key, w_value,
    persist_keys, persist_values, w_out, mem_query, mem_key, mem_value, mem_first, mem_second,
    ffn_gain, w_gate, w_up, w_down, cotangent,
):
    ctx = lax.axis_size("ctx")
    shard = lax.axis_size("shard")
    me = lax.axis_index("ctx")
    rows, width = block_input.shape[1:]
    total = rows * ctx
    part = width // ctx
    hidden = w_gate.shape[1]
    wrows = w_query.shape[0]
    drows = w_down.shape[0]
    dpart = drows // ctx
    fpart = dpart * shard
    heads = HEADS // ctx
    persist = persist_keys.shape[0]
    chunks = total // SPAN

    def mine(w, size):
        return lax.dynamic_slice_in_dim(w, me * size, size, 1)

    def mine_ffn(w):
        return lax.dynamic_index_in_dim(w.reshape(w.shape[0], shard, ctx, dpart), me, 2, keepdims=False).reshape(w.shape[0], fpart)

    def full_weights(group):
        local = jnp.concatenate(group, axis=1)
        quarter = lax.dynamic_slice_in_dim(local, me * (wrows // ctx), wrows // ctx, 0)
        got = gather_shard(quarter).reshape(shard * (wrows // ctx), -1)
        got = gather_ctx(got).reshape(ctx, shard, wrows // ctx, -1)
        got = jnp.swapaxes(got, 0, 1).reshape(shard * wrows, -1)
        return [got[:, k * width : (k + 1) * width] for k in range(len(group))]

    small = jnp.concatenate([persist_keys, persist_values, norm_gain[None], ffn_gain[None]], 0)
    small = jnp.swapaxes(gather_shard(small), 0, 1).reshape(2 * persist + 2, width)
    p_keys = mine(small[:persist], part)
    p_values = mine(small[persist : 2 * persist], part)
    gain_one = small[2 * persist].astype(f32)[None]
    gain_two = small[2 * persist + 1].astype(f32)[None]

    scalars = jnp.concatenate([mem_keep, mem_momentum, mem_rate], 0).T
    scalars = gather_ctx(scalars)
    a_tab, b_tab = tables(scalars[:, 0], scalars[:, 1], scalars[:, 2])
    tokens_low = gather_ctx(block_input[0])
    mk_w, first_w = full_weights([mem_key, mem_first])
    mv_w, second_w = full_weights([mem_value, mem_second])
    qkv = gather_shard(jnp.concatenate([mine(w_query, part), mine(w_key, part), mine(w_value, part)], 1)).reshape(width, 3 * part)
    mq_w, out_w = full_weights([mem_query, w_out])
    gateup = gather_shard(jnp.concatenate([mine_ffn(w_gate), mine_ffn(w_up)], 1)).reshape(width, 2 * fpart)
    down = gather_shard(lax.dynamic_slice_in_dim(w_down, me * dpart, dpart, 0)).reshape(fpart, width)
    cot_low = gather_ctx(cotangent[0])

    length = lengths[0]
    slots = jnp.arange(total, dtype=jnp.int32)
    alive = (slots < length).astype(f32)[:, None]
    tokens = tokens_low.astype(f32)
    root_one = rms_rows(tokens)
    normed = (tokens * root_one * gain_one).astype(bf16)
    mkey = dot(normed, mk_w).astype(bf16)
    mvalue = dot(normed, mv_w).astype(bf16)
    mquery = dot(normed, mq_w).astype(bf16)
    a_rows = jnp.repeat(a_tab, SPAN)[:, None]
    b_all = jnp.repeat(jnp.repeat(b_tab, SPAN, axis=0), SPAN, axis=1)

    qkv_rows = dot(normed, qkv).astype(bf16)
    q = qkv_rows[:, :part].reshape(total, heads, HEAD_DIM)
    k = jnp.concatenate([p_keys, qkv_rows[:, part : 2 * part]], 0).reshape(-1, heads, HEAD_DIM)
    v = jnp.concatenate([p_values, qkv_rows[:, 2 * part :]], 0).reshape(-1, heads, HEAD_DIM)
    scale = HEAD_DIM ** (-0.5)
    window_ok = (slots[None, :] <= slots[:, None]) & (slots[:, None] - slots[None, :] < WINDOW) & (slots[None, :] < length)
    allowed = jnp.concatenate([jnp.ones((total, persist), dtype=bool), window_ok], 1)
    scores = jnp.einsum("thd,shd->hts", q, k, preferred_element_type=f32) * scale
    scores = jnp.where(allowed[None], scores, -1e30)
    peak = jnp.max(scores, axis=-1, keepdims=True)
    expo = jnp.exp(scores - peak)
    probs_f = expo / jnp.sum(expo, axis=-1, keepdims=True)
    probs = probs_f.astype(bf16)
    attended_mine = jnp.einsum("hts,shd->thd", probs, v, preferred_element_type=f32).reshape(total, part)
    att = gather_ctx(attended_mine.astype(bf16)[None]).swapaxes(0, 1).reshape(total, width).astype(f32)

    def blk(arr, c):
        return arr[c * SPAN : (c + 1) * SPAN]

    key_first = dot(mkey, first_w)
    kk = b_all * dot_t(mkey, mkey)
    kk = kk.astype(bf16)
    z_l, h_l, e_l, u_l, g_l = [], [], [], [], []
    hcat = ecat = gcat = None
    for c in range(chunks):
        z = a_tab[c] * blk(key_first, c)
        if c:
            z = z - dot(blk(kk, c)[:, : c * SPAN], gcat)
        h, slope, _ = silu_parts(z)
        hb = h.astype(bf16)
        pred = a_tab[c] * dot(hb, second_w)
        if c:
            bc = blk(b_all, c)[:, : c * SPAN]
            pred = pred - dot((bc * dot_t(hb, hcat)).astype(bf16), ecat)
        err = blk(alive, c) * (pred - blk(mvalue, c).astype(f32)) / SPAN
        eb = err.astype(bf16)
        u = a_tab[c] * dot_t(eb, second_w)
        if c:
            u = u - dot((bc * dot_t(eb, ecat)).astype(bf16), hcat)
        gb = (u * slope).astype(bf16)
        hcat = hb if c == 0 else jnp.concatenate([hcat, hb], 0)
        ecat = eb if c == 0 else jnp.concatenate([ecat, eb], 0)
        gcat = gb if c == 0 else jnp.concatenate([gcat, gb], 0)
        z_l.append(z)
        u_l.append(u)
    kq = (b_all * dot_t(mquery, mkey)).astype(bf16)
    zq = a_rows * dot(mquery, first_w) - dot(kq, gcat)
    hq, slope_q, _ = silu_parts(zq)
    hqb = hq.astype(bf16)
    hqh = (b_all * dot_t(hqb, hcat)).astype(bf16)
    recalled = a_rows * dot(hqb, second_w) - dot(hqh, ecat)

    combined = (att * recalled).astype(bf16)
    middle = tokens + dot(combined, out_w)
    root_two = rms_rows(middle)
    normed_two = (middle * root_two * gain_two).astype(bf16)
    gu = dot(normed_two, gateup)
    gate, up = gu[:, :fpart], gu[:, fpart:]
    act, gate_slope, _ = silu_parts(gate)
    activated = (act * up).astype(bf16)
    ffn_own = reduce_ctx(dot(activated, down))
    mid_own = lax.dynamic_slice_in_dim(middle, me * rows, rows, 0)
    alive_own = lax.dynamic_slice_in_dim(alive, me * rows, rows, 0)
    result = alive_own * (mid_own + ffn_own)

    d_ffn = (cot_low.astype(f32) * alive).astype(bf16)
    d_result = d_ffn.astype(f32)
    g_down = t_dot(activated, d_ffn)
    d_act = dot_t(d_ffn, down)
    d_gate = (d_act * up * gate_slope).astype(bf16)
    d_up = (d_act * act).astype(bf16)
    d_gu = jnp.concatenate([d_gate, d_up], 1)
    g_gu = t_dot(normed_two, d_gu)
    d_normed_two = gather_ctx(reduce_ctx(dot_t(d_gu, gateup)).astype(bf16)).astype(f32)
    d_norm, g_gain_two = rms_back(middle, root_two, gain_two, d_normed_two)
    d_middle = d_result + d_norm
    d_branch = d_middle.astype(bf16)
    g_out = t_dot(mine(combined, part), d_branch)
    d_combined = dot_t(d_branch, out_w)
    d_att = (mine(d_combined, part) * mine(recalled, part)).astype(bf16)
    d_rec = (d_combined * att).astype(bf16)

    d_heads = d_att.reshape(total, heads, HEAD_DIM)
    d_probs = jnp.einsum("thd,shd->hts", d_heads, v, preferred_element_type=f32)
    centre = jnp.sum(d_probs * probs_f, axis=-1, keepdims=True)
    d_scores = (probs_f * (d_probs - centre)).astype(bf16)
    d_q = (scale * jnp.einsum("hts,shd->thd", d_scores, k, preferred_element_type=f32)).reshape(total, part)
    d_k = (scale * jnp.einsum("hts,thd->shd", d_scores, q, preferred_element_type=f32)).reshape(-1, part)
    d_v = jnp.einsum("hts,thd->shd", probs, d_heads, preferred_element_type=f32).reshape(-1, part)
    g_pkeys, g_pvalues = d_k[:persist], d_v[:persist]
    d_qkv = jnp.concatenate([d_q, d_k[persist:], d_v[persist:]], 1).astype(bf16)
    g_qkv = t_dot(normed, d_qkv)
    d_normed_qkv = reduce_ctx(dot_t(d_qkv, qkv))

    dh_q = a_rows * dot_t(d_rec, second_w)
    n1 = (b_all * dot_t(d_rec, ecat)).astype(bf16)
    dh_q = dh_q - dot(n1, hcat)
    dz_q = (dh_q * slope_q).astype(bf16)
    d_e = -t_dot(hqh, d_rec)
    d_h = -t_dot(n1, hqb)
    d_g = -t_dot(kq, dz_q)
    n2 = (b_all * dot_t(dz_q, gcat)).astype(bf16)
    d_mq = a_rows * dot_t(dz_q, first_w) - dot(n2, mkey)
    d_mk = -t_dot(n2, mquery)
    dz_l, du_l, dp_l = [None] * chunks, [None] * chunks, [None] * chunks
    for c in range(chunks - 1, -1, -1):
        lo = c * SPAN
        z, u = z_l[c], u_l[c]
        _, slope, bend = silu_parts(z)
        hb, eb = blk(hcat, c), blk(ecat, c)
        dg = blk(d_g, c)
        du = dg * slope
        dz = dg * u * bend
        dub = du.astype(bf16)
        de = blk(d_e, c) + a_tab[c] * dot(dub, second_w)
        if c:
            bc = blk(b_all, c)[:, :lo]
            hl, el = hcat[:lo], ecat[:lo]
            n3 = (bc * dot_t(dub, hl)).astype(bf16)
            m3 = (bc * dot_t(eb, el)).astype(bf16)
            de = de - dot(n3, el)
        dp = blk(alive, c) * de / SPAN
        dpb = dp.astype(bf16)
        dh = blk(d_h, c) + a_tab[c] * dot_t(dpb, second_w)
        if c:
            n4 = (bc * dot_t(dpb, el)).astype(bf16)
            m4 = (bc * dot_t(hb, hl)).astype(bf16)
            dh = dh - dot(n4, hl)
        dz = dz + dh * slope
        dzb = dz.astype(bf16)
        if c:
            m5 = blk(kk, c)[:, :lo]
            d_h = d_h[:lo] - t_dot(jnp.concatenate([m3, n4], 0), jnp.concatenate([dub, hb], 0))
            d_e = d_e[:lo] - t_dot(jnp.concatenate([n3, m4], 0), jnp.concatenate([eb, dpb], 0))
            d_g = d_g[:lo] - t_dot(m5, dzb)
        dz_l[c], du_l[c], dp_l[c] = dzb, dub, dp
    dz = jnp.concatenate(dz_l, 0)
    du = jnp.concatenate(du_l, 0)
    dp = jnp.concatenate(dp_l, 0)
    d_mv = (-dp).astype(bf16)
    n5 = (b_all * dot_t(dz, gcat)).astype(bf16)
    d_mk = d_mk + a_rows * dot_t(dz, first_w) - dot(n5, mkey) - t_dot(n5, mkey)
    d_mk = d_mk.astype(bf16)
    d_mq = d_mq.astype(bf16)

    def scaled(arr):
        return (a_rows * arr.astype(f32)).astype(bf16)

    g_first = t_dot(mine(mkey, part), scaled(dz)) + t_dot(mine(mquery, part), scaled(dz_q))
    g_second = t_dot(mine(hcat, part), scaled(dp)) + t_dot(mine(hqb, part), scaled(d_rec)) + t_dot(mine(du, part), scaled(ecat))
    normed_mine = mine(normed, part)
    g_mq = t_dot(normed_mine, d_mq)
    g_mk = t_dot(normed_mine, d_mk)
    g_mv = t_dot(normed_mine, d_mv)

    def own(arr):
        return lax.dynamic_slice_in_dim(arr, me * rows, rows, 0)

    d_normed = d_normed_qkv + dot_t(own(d_mq), mq_w) + dot_t(own(d_mk), mk_w) + dot_t(own(d_mv), mv_w)
    d_tok, g_gain_one = rms_back(own(tokens), own(root_one), gain_one, d_normed)
    input_grad = own(d_middle) + d_tok

    each = width // (ctx * shard)
    by_rows = jnp.concatenate([g_out, g_mq, g_mk, g_mv, g_first, g_second], 1)
    by_rows = reduce_shard(by_rows.reshape(shard, each, -1))
    by_rows = [by_rows[:, i * width : (i + 1) * width] for i in range(6)]
    columns = jnp.concatenate([g_qkv, g_gu], 1).reshape(ctx, shard, each, -1)
    columns = reduce_shard(jnp.swapaxes(columns, 0, 1))
    columns = lax.all_to_all(columns, "ctx", 0, 0)
    g_q, g_k, g_v = [
        jnp.swapaxes(columns[:, :, i * part : (i + 1) * part], 0, 1).reshape(each, width) for i in range(3)
    ]

    def ffn_columns(begin):
        taken = columns[:, :, begin : begin + fpart].reshape(ctx, each, shard, dpart)
        return jnp.transpose(taken, (1, 2, 0, 3)).reshape(each, hidden)

    g_gate = ffn_columns(3 * part)
    g_up = ffn_columns(3 * part + fpart)
    g_down = reduce_shard(g_down.reshape(shard, dpart, width))
    pairs = []
    for i in range(ctx):
        for s in range(shard):
            pairs.append((i * shard + s, s * ctx + i))
    g_down = lax.ppermute(g_down, ("ctx", "shard"), pairs)

    def narrow(arr):
        return jnp.swapaxes(arr.reshape(arr.shape[0], shard, each), 0, 1)

    gain_one_all = lax.psum(g_gain_one, ("ctx", "shard"))
    tiny = jnp.concatenate([g_pkeys, g_pvalues, mine(g_gain_two[None], part)], 0)
    tiny = lax.psum(tiny, "shard")
    s_me = lax.axis_index("shard")
    tiny = lax.dynamic_slice_in_dim(tiny, s_me * each, each, 1)
    gain_one_out = lax.dynamic_slice_in_dim(gain_one_all, (me * shard + s_me) * each, each, 0)
    return (
        result.astype(bf16)[None],
        input_grad.astype(bf16)[None],
        gain_one_out,
        g_q, g_k, g_v,
        tiny[:persist], tiny[persist : 2 * persist],
        by_rows[0], by_rows[1], by_rows[2], by_rows[3], by_rows[4], by_rows[5],
        tiny[2 * persist],
        g_gate, g_up, g_down,
    )


def solution(mesh):
    row = P("shard", None)
    col = P(None, "shard")
    vec = P("shard")
    seq = P("shard", "ctx", None)
    sc = P("shard", "ctx")
    in_specs = (
        seq, vec, sc, sc, sc, vec, row, row, row, col, col, row, row, row, row, row, row, vec, row, row, row, seq,
    )
    both = ("ctx", "shard")
    orow = P(both, None)
    out_specs = (
        seq, seq, P(both), orow, orow, orow, P(None, both), P(None, both), orow, orow, orow, orow, orow, orow,
        P(both), orow, orow, orow,
    )
    return jax.shard_map(on_device, mesh=mesh, in_specs=in_specs, out_specs=out_specs, check_vma=False)
```
